128 devices in a mesh: judge: 4 (over y_hi, core), fsdp: 32 (over y_lo, x, z).
Axes of the slice: x: 4, y: 4 (y_hi: 2, y_lo: 2; y = y_hi * 2 + y_lo), z: 4, core: 2. Of those that a mesh axis runs over, the one named last changes fastest.
Arguments:
- hidden: bfloat16 [4, 32768, 4096], P('judge', 'fsdp'), may hold values from -32 to 32
- lengths: int32 [64], replicated, may hold values from 128 to 512
- duplicate_group_index: int32 [64], replicated, may hold values from 0 to 15, as said below
- attn_gain: bfloat16 [4, 4096], P('judge', 'fsdp'), may hold values from 0.5 to 1.5
- w_query: bfloat16 [4, 4096, 4096], P('judge', None, 'fsdp'), may hold values from -1 to 1
- w_key: bfloat16 [4, 4096, 1024], P('judge', 'fsdp'), may hold values from -1 to 1
- w_value: bfloat16 [4, 4096, 1024], P('judge', 'fsdp'), may hold values from -0.09375 to 0.09375
- w_out: bfloat16 [4, 4096, 4096], P('judge', 'fsdp'), may hold values from -0.09375 to 0.09375
- mlp_gain: bfloat16 [4, 4096], P('judge', 'fsdp'), may hold values from 0.5 to 1.5
- w_gate: bfloat16 [4, 4096, 14336], P('judge', None, 'fsdp'), may hold values from -0.09375 to 0.09375
- w_up: bfloat16 [4, 4096, 14336], P('judge', None, 'fsdp'), may hold values from -0.09375 to 0.09375
- w_down: bfloat16 [4, 14336, 4096], P('judge', 'fsdp'), may hold values from -0.046875 to 0.046875
- final_gain: bfloat16 [4, 4096], P('judge', 'fsdp'), may hold values from 0.5 to 1.5
- reward_head: float32 [4, 4096], P('judge'), may hold values from -8 to 8
Outputs:
- survivor_weights: float32 [64], replicated
- cluster_features: float32 [16, 4096], P(None, 'fsdp')
The draws below stay inside these ranges and needn't reach their ends.
Inputs may be any that keep to these rules, and one draw needn't show every extreme that they name: `duplicate_group_index`: every cluster holds exactly four candidates.
All inputs are finite; a program needn't handle non-finite values.
Results may differ from the reference program's by a relative error of at most 0.003.
Values may be sent and summed in bfloat16 or wider, within the bound.
No kernel may reach another device: no remote copies, remote signals or barrier semaphores. Data moves between devices by JAX's collectives and lax.ppermute only.
A program may use at most 192 MiB of HBM per device.

```python
import math
import jax
import jax.numpy as jnp
from jax import lax

D = 4096
HEADS = 32
KV_HEADS = 8
HEAD_DIM = 128
FF = 14336
LEN = 512
JUDGES = 4
CANDS = 64
TOKENS = 32768
DUPLICATE_GROUPS = 16
KVW = 1024
N_JUDGE = 4


def column_profile(ratio):
    position = jnp.arange(D, dtype=jnp.float32) / (D - 1)
    return jnp.exp(math.log(ratio) * (position - 0.5))


def cluster_law(key):
    shuffled = jax.random.permutation(jax.random.fold_in(key, 101), CANDS)
    return (shuffled % DUPLICATE_GROUPS).astype(jnp.int32)


def draw_duplicate_group_index(key, part):
    return cluster_law(key)


def draw_hidden(key, part):
    base_noise = jax.random.truncated_normal(jax.random.fold_in(key, 1), -4.5, 4.5, (JUDGES, TOKENS, D), jnp.float32)
    values = base_noise * column_profile(10.0)[None, None, :]
    return values.astype(jnp.bfloat16)


def draw_w_query(key, part):
    matrix = jax.random.truncated_normal(jax.random.fold_in(key, 11), -4.0, 4.0, (JUDGES, D, D), jnp.float32) / math.sqrt(D)
    return matrix.astype(jnp.bfloat16)


def draw_w_key(key, part):
    matrix = jax.random.truncated_normal(jax.random.fold_in(key, 17), -4.0, 4.0, (JUDGES, D, KVW), jnp.float32) / math.sqrt(D)
    return matrix.astype(jnp.bfloat16)


def draw_reward_head(key, part):
    matrix = jax.random.truncated_normal(jax.random.fold_in(key, 21), -4.0, 4.0, (JUDGES, D), jnp.float32) / math.sqrt(D // 4)
    return matrix.astype(jnp.float32)


def set_ends(entries, key, smallest, largest):
    longest = entries.shape.index(max(entries.shape))
    spots = []
    for shift in (0, 1):
        where = [jax.random.randint(jax.random.fold_in(key, axis), (), 0, length) for axis, length in enumerate(entries.shape)]
        where[longest] = (where[longest] + shift) % entries.shape[longest]
        spots.append(tuple(where))
    return entries.at[spots[0]].set(smallest).at[spots[1]].set(largest)


def block_scale(key, dims, cuts, least, high):
    def one(axis_at, parts):
        steps = jax.random.uniform(jax.random.fold_in(jax.random.fold_in(key, 6), axis_at), (parts,), jnp.float32, least / len(cuts), high / len(cuts))
        return jnp.repeat(jnp.exp(steps), dims[axis_at] // parts).reshape((-1,) + (1,) * (len(dims) - axis_at - 1))

    level = one(*cuts[0])
    for cut in cuts[1:]:
        level = level * one(*cut)
    return level


def noise(rng, extent, scale, limit, cuts=(), kind=jnp.bfloat16):
    loudness = block_scale(rng, extent, cuts, -0.22, 0.18) if cuts else 1.0
    values = jax.random.normal(rng, extent, jnp.float32) * scale * loudness
    return jnp.minimum(jnp.maximum(values, -limit), limit).astype(kind)


def setup_inputs(seed: int = 0) -> dict:
    streams_of = jax.random.split(jax.random.key(seed), 15)
    hidden = draw_hidden(jax.random.fold_in(streams_of[14], 71), 0)
    lengths = set_ends(jax.random.randint(streams_of[1], (CANDS,), LEN // 4, LEN + 1), jax.random.fold_in(streams_of[1], 1), LEN // 4, LEN).astype(jnp.int32)
    duplicate_group_index = draw_duplicate_group_index(jax.random.fold_in(streams_of[14], 71), 0)
    attn_gain = jnp.clip(1.0 + 0.1 * jax.random.normal(streams_of[3], (JUDGES, D), jnp.float32), 0.5, 1.5).astype(jnp.bfloat16)
    w_query = draw_w_query(jax.random.fold_in(streams_of[14], 71), 0)
    w_key = draw_w_key(jax.random.fold_in(streams_of[14], 71), 0)
    w_value = noise(streams_of[6], (JUDGES, D, KVW), D ** -0.5, 0.09375, ((0, 4), (1, 32)))
    w_out = noise(streams_of[7], (JUDGES, D, D), D ** -0.5, 0.09375, ((0, 4), (1, 32)))
    mlp_gain = jnp.clip(1.0 + 0.1 * jax.random.normal(streams_of[8], (JUDGES, D), jnp.float32), 0.5, 1.5).astype(jnp.bfloat16)
    w_gate = noise(streams_of[9], (JUDGES, D, FF), D ** -0.5, 0.09375, ((0, 4), (2, 32)))
    w_up = noise(streams_of[10], (JUDGES, D, FF), D ** -0.5, 0.09375, ((0, 4), (2, 32)))
    w_down = noise(streams_of[11], (JUDGES, FF, D), FF ** -0.5, 0.046875, ((0, 4), (1, 32)))
    final_gain = jnp.clip(1.0 + 0.1 * jax.random.normal(streams_of[12], (JUDGES, D), jnp.float32), 0.5, 1.5).astype(jnp.bfloat16)
    reward_head = draw_reward_head(jax.random.fold_in(streams_of[14], 71), 0)
    return {"hidden": hidden, "lengths": lengths, "duplicate_group_index": duplicate_group_index, "attn_gain": attn_gain, "w_query": w_query, "w_key": w_key, "w_value": w_value, "w_out": w_out, "mlp_gain": mlp_gain, "w_gate": w_gate, "w_up": w_up, "w_down": w_down, "final_gain": final_gain, "reward_head": reward_head}


EPS = 1e-05
ROPE_BASE = 500000.0

def normalize(v, gain):
    v = v.astype(jnp.float32)
    return v * lax.rsqrt(lax.optimization_barrier(jnp.mean(v * v, axis=-1, keepdims=True)) + EPS) * gain.astype(jnp.float32)

def angles(position):
    half = HEAD_DIM // 2
    freq = jnp.exp(jnp.arange(half, dtype=jnp.float32) * (-2.0 * math.log(ROPE_BASE) / HEAD_DIM))
    turned = position[..., None] * freq
    return (jnp.cos(turned), jnp.sin(turned))

def rotate(v, cosine, sine):
    half = HEAD_DIM // 2
    first = v[..., :half]
    second = v[..., half:]
    return jnp.concatenate([first * cosine - second * sine, second * cosine + first * sine], axis=-1)

def judge_features(x, lengths, attn_gain, w_query, w_key, w_value, w_out, mlp_gain, w_gate, w_up, w_down, final_gain):
    groups = HEADS // KV_HEADS
    last_index = jnp.arange(CANDS, dtype=jnp.int32) * LEN + lengths - 1
    x_last = x[last_index].astype(jnp.float32)
    q_norm = normalize(x_last, attn_gain).astype(jnp.bfloat16)
    query = jnp.dot(q_norm, w_query, preferred_element_type=jnp.float32).reshape(CANDS, HEADS, HEAD_DIM)
    cosine, sine = angles((lengths - 1).astype(jnp.float32))
    query = rotate(query, cosine[:, None, :], sine[:, None, :]).astype(jnp.bfloat16)
    query = query.reshape(CANDS, KV_HEADS, groups, HEAD_DIM)
    key_cos, key_sin = angles(jnp.arange(LEN, dtype=jnp.float32))
    blocks = x.reshape(CANDS, LEN, D)

    def attend(item):
        block, q_one, length = item
        tok_norm = normalize(block, attn_gain).astype(jnp.bfloat16)
        keys = jnp.dot(tok_norm, w_key, preferred_element_type=jnp.float32).reshape(LEN, KV_HEADS, HEAD_DIM)
        keys = rotate(keys, key_cos[:, None, :], key_sin[:, None, :]).astype(jnp.bfloat16)
        values = jnp.dot(tok_norm, w_value, preferred_element_type=jnp.float32).astype(jnp.bfloat16)
        values = values.reshape(LEN, KV_HEADS, HEAD_DIM)
        scores = jnp.einsum('kgd,lkd->kgl', q_one.astype(jnp.float32), keys.astype(jnp.float32)) * HEAD_DIM ** (-0.5)
        valid = jnp.arange(LEN, dtype=jnp.int32) < length
        scores = jnp.where(valid, scores, -1e+30)
        top = lax.optimization_barrier(jnp.max(scores, axis=-1, keepdims=True))
        expo = jnp.exp(scores - top)
        probs = (expo / lax.optimization_barrier(jnp.sum(expo, axis=-1, keepdims=True))).astype(jnp.bfloat16)
        mixed = jnp.einsum('kgl,lkd->kgd', probs.astype(jnp.float32), values.astype(jnp.float32))
        return mixed.reshape(D).astype(jnp.bfloat16)
    mixed = lax.map(attend, (blocks, query, lengths))
    after_attn = x_last + jnp.dot(mixed, w_out, preferred_element_type=jnp.float32)
    m_norm = normalize(after_attn, mlp_gain).astype(jnp.bfloat16)
    gate = jnp.dot(m_norm, w_gate, preferred_element_type=jnp.float32)
    up = jnp.dot(m_norm, w_up, preferred_element_type=jnp.float32)
    act = (jax.nn.silu(gate) * up).astype(jnp.bfloat16)
    after_mlp = after_attn + jnp.dot(act, w_down, preferred_element_type=jnp.float32)
    return normalize(after_mlp, final_gain)

def remaining_candidates(judge_panel, duplicate_group_index, duplicate_groups):
    same = duplicate_group_index[:, None] == duplicate_group_index[None, :]
    top = lax.optimization_barrier(jnp.max(jnp.where(same, judge_panel[None, :], -1e+30), axis=1))
    expo = jnp.exp(judge_panel - top)
    total = lax.optimization_barrier(jnp.sum(jnp.where(same, expo[None, :], 0.0), axis=1))
    weight_values = expo / total
    panel_member = (duplicate_group_index[:, None] == jnp.arange(duplicate_groups, dtype=jnp.int32)[None, :]).astype(jnp.float32)
    return (weight_values, panel_member)

def reference(hidden, lengths, duplicate_group_index, attn_gain, w_query, w_key, w_value, w_out, mlp_gain, w_gate, w_up, w_down, final_gain, reward_head):
    total_features = jnp.zeros((CANDS, D), jnp.float32)
    score_total = jnp.zeros((CANDS,), jnp.float32)
    for judge in range(N_JUDGE):
        features = judge_features(hidden[judge], lengths, attn_gain[judge], w_query[judge], w_key[judge], w_value[judge], w_out[judge], mlp_gain[judge], w_gate[judge], w_up[judge], w_down[judge], final_gain[judge])
        score = jnp.dot(features, reward_head[judge], precision=lax.Precision.HIGHEST)
        total_features = total_features + features
        score_total = score_total + score
    mean_features = total_features / N_JUDGE
    judge_panel = score_total / N_JUDGE
    weight_values, panel_member = remaining_candidates(judge_panel, duplicate_group_index, DUPLICATE_GROUPS)
    cluster_features = jnp.dot(panel_member.T, weight_values[:, None] * mean_features, precision=lax.Precision.HIGHEST)
    return (weight_values, cluster_features)
```

```python
import math

import jax
import jax.numpy as jnp
from jax import lax
from jax.experimental import pallas as pl
from jax.experimental.pallas import tpu as pltpu
from jax.sharding import PartitionSpec as P


KV_HEADS = 8
HEAD_DIM = 128
LEN = 512
EPS = 1e-05
ROPE_BASE = 500000.0
NY, NX, NZ = 2, 4, 4
GROUP = NY * NX * NZ


OWN_LIMIT = 16 << 20
SMALL_LIMIT = 12 << 20
NEAR_LIMIT = 16 << 20
ATTEND_LIMIT = 20 << 20


def place(y, x, z):
    return ((y % NY) * NX + x % NX) * NZ + z % NZ


def moved(v, dy=0, dx=0, dz=0):
    pairs = [
        (place(y, x, z), place(y + dy, x + dx, z + dz))
        for y in range(NY)
        for x in range(NX)
        for z in range(NZ)
    ]
    return lax.ppermute(v, "fsdp", pairs)


def along(v, name, step):
    return moved(v, **{name: step})


def small_ring(v, name):
    after = along(v, name, -1)
    before = along(v, name, 1)
    opposite = along(v, name, 2)
    return jnp.stack([v, after]), jnp.stack([opposite, before])


def large_ring(low, high, name):
    before_low = along(low, name, 1)
    after_high = along(high, name, -1)
    before_high = along(high, name, 1)
    after_low = along(low, name, -1)
    far = (along(before_low, name, 1), along(after_high, name, -1))
    return (after_low, after_high, before_low, before_high), far


def exchanged(x, axis):
    return lax.all_to_all(x, axis, 0, 0, tiled=True)


def row_scale(v):
    return lax.rsqrt(jnp.mean(v * v, axis=-1, keepdims=True) + EPS)


def angles(position):
    half = HEAD_DIM // 2
    freq = jnp.exp(jnp.arange(half, dtype=jnp.float32) * (-2.0 * math.log(ROPE_BASE) / HEAD_DIM))
    turned = position[..., None] * freq
    return (jnp.cos(turned), jnp.sin(turned))


def rotate(v, cosine, sine):
    half = HEAD_DIM // 2
    first = v[..., :half]
    second = v[..., half:]
    return jnp.concatenate(
        [first * cosine - second * sine, second * cosine + first * sine], axis=-1
    )


def column_of(pos_ref, zo, xo, yo):
    y = lax.rem(pos_ref[0] + yo, NY)
    x = lax.rem(pos_ref[1] + xo, NX)
    z = lax.rem(pos_ref[2] + zo, NZ)
    return pl.multiple_of(((y * NX + x) * NZ + z) * 128, 128)


def pack_kernel(dev_ref, len_ref, x0_ref, x1_ref, ga_ref, gm_ref, gf_ref, out_ref, own_ref):
    width = x0_ref.shape[1]
    peers = out_ref.shape[0]
    rows = []
    for i, x_ref in enumerate((x0_ref, x1_ref)):
        slot = lax.rem(len_ref[2 * dev_ref[0] + i] - 1, 16)
        x = x_ref[...].astype(jnp.float32)
        own = lax.broadcasted_iota(jnp.int32, x.shape, 0) == slot
        rows.append(jnp.sum(jnp.where(own, x, 0.0), axis=0, keepdims=True))
    own_ref[...] = jnp.concatenate(rows, axis=0)
    gains = [g[...].astype(jnp.float32) for g in (ga_ref, gm_ref, gf_ref)]
    first = jnp.concatenate([rows[0], gains[0], gains[2]], axis=1)
    second = jnp.concatenate([rows[1], gains[1], gains[1]], axis=1)
    both = jnp.concatenate([first, second], axis=0).astype(jnp.bfloat16)
    out_ref[...] = jnp.broadcast_to(both[None], (peers, 2, width + 256))


def pack_last(dev, lengths, tokens, attn_gain, mlp_gain, final_gain, peers):
    width = tokens.shape[1]

    def row_block(i):
        return pl.BlockSpec(
            (16, width), lambda s, d, n: ((i * LEN + n[2 * d[0] + i] - 1) // 16, 0)
        )

    gain = pl.BlockSpec((1, 128), lambda s, d, n: (0, 0))
    return pl.pallas_call(
        pack_kernel,
        out_shape=(
            jax.ShapeDtypeStruct((peers, 2, width + 256), jnp.bfloat16),
            jax.ShapeDtypeStruct((2, width), jnp.float32),
        ),
        grid_spec=pltpu.PrefetchScalarGridSpec(
            num_scalar_prefetch=2,
            grid=(1,),
            in_specs=[row_block(0), row_block(1), gain, gain, gain],
            out_specs=(
                pl.BlockSpec((peers, 2, width + 256), lambda s, d, n: (0, 0, 0)),
                pl.BlockSpec((2, width), lambda s, d, n: (0, 0)),
            ),
        ),
        name="pack_last",
    )(dev, lengths, tokens, tokens, attn_gain, mlp_gain, final_gain)


def columns(x_ref, rows, dev_ref, blocks):
    parts = []
    for zo, xo in blocks:
        for yo in range(NY):
            parts.append(x_ref[rows, pl.ds(column_of(dev_ref, zo, xo, yo), 128)])
    return jnp.concatenate(parts, axis=1)


def times(lhs, low, high):
    half = lhs.shape[1] // 2
    return jnp.dot(
        lhs[:, :half], low[...].reshape(half, -1), preferred_element_type=jnp.float32
    ) + jnp.dot(lhs[:, half:], high[...].reshape(half, -1), preferred_element_type=jnp.float32)


def z_group(off):
    return [(off, i) for i in range(NX)]


def x_group(off):
    return [(i, off) for i in range(NZ)]


ROWS = 256
VMEM = pl.BlockSpec(memory_space=pltpu.VMEM)
SMEM = pl.BlockSpec(memory_space=pltpu.SMEM)


def own_keys_kernel(dev_ref, hbm_ref, a_low, a_high, b_low, b_high, out_ref, sum_ref, x_ref, sems):
    steps = hbm_ref.shape[0] // ROWS
    copies = []
    for i in range(steps):
        rows = pl.ds(i * ROWS, ROWS)
        copies.append(pltpu.make_async_copy(hbm_ref.at[rows], x_ref.at[rows], sems.at[i]))
        copies[i].start()
    for i in range(steps):
        rows = pl.ds(i * ROWS, ROWS)
        copies[i].wait()
        out_ref[rows, :512] = times(columns(x_ref, rows, dev_ref, z_group(0)), a_low, a_high)
        out_ref[rows, 512:] = times(columns(x_ref, rows, dev_ref, x_group(0)), b_low, b_high)
        x = x_ref[rows, :].astype(jnp.float32)
        sum_ref[rows, :] = jnp.broadcast_to(jnp.sum(x * x, axis=1, keepdims=True), (ROWS, 128))


def near_keys_kernel(dev_ref, x_ref, acc_ref, a1l, a1h, a3l, a3h, b1l, b1h, b3l, b3h, out_ref):
    def step(i, carry):
        rows = pl.ds(pl.multiple_of(i * ROWS, ROWS), ROWS)
        first = acc_ref[rows, :512]
        first += times(columns(x_ref, rows, dev_ref, z_group(1)), a1l, a1h)
        first += times(columns(x_ref, rows, dev_ref, z_group(3)), a3l, a3h)
        out_ref[rows, :512] = first
        second = acc_ref[rows, 512:]
        second += times(columns(x_ref, rows, dev_ref, x_group(1)), b1l, b1h)
        second += times(columns(x_ref, rows, dev_ref, x_group(3)), b3l, b3h)
        out_ref[rows, 512:] = second
        return carry

    lax.fori_loop(0, x_ref.shape[0] // ROWS, step, 0)


def own_keys(dev, tokens, parts):
    rows = tokens.shape[0]
    return pl.pallas_call(
        own_keys_kernel,
        out_shape=(
            jax.ShapeDtypeStruct((rows, 1024), jnp.float32),
            jax.ShapeDtypeStruct((rows, 128), jnp.float32),
            jax.ShapeDtypeStruct(tokens.shape, tokens.dtype),
        ),
        in_specs=[SMEM, pl.BlockSpec(memory_space=pltpu.HBM)] + [VMEM] * 4,
        out_specs=(VMEM, VMEM, VMEM),
        scratch_shapes=[pltpu.SemaphoreType.DMA((rows // ROWS,))],
        compiler_params=pltpu.CompilerParams(vmem_limit_bytes=OWN_LIMIT),
        name="own_keys",
    )(dev, pltpu.with_memory_space_constraint(tokens, pltpu.HBM), *parts)


def near_keys(dev, tokens, acc, parts):
    return pl.pallas_call(
        near_keys_kernel,
        out_shape=jax.ShapeDtypeStruct(acc.shape, jnp.float32),
        in_specs=[SMEM] + [VMEM] * 10,
        out_specs=VMEM,
        input_output_aliases={2: 0},
        compiler_params=pltpu.CompilerParams(vmem_limit_bytes=NEAR_LIMIT),
        name="near_keys",
    )(dev, tokens, acc, *parts)


def attend_kernel(
    dev_ref,
    len_ref,
    x_ref,
    acc_ref,
    sum_ref,
    a_low,
    a_high,
    b_low,
    b_high,
    q_ref,
    cos_ref,
    sin_ref,
    out_ref,
):
    width = x_ref.shape[1]
    heads = q_ref.shape[0] * 2
    per_key = heads // KV_HEADS
    cosine = cos_ref[...]
    sine = sin_ref[...]
    q = q_ref[:, :2, :].reshape(heads, HEAD_DIM)
    chosen = []
    for c in range(2):
        rows = pl.ds(c * LEN, LEN)
        halves = (
            acc_ref[rows, :512] + times(columns(x_ref, rows, dev_ref, z_group(2)), a_low, a_high),
            acc_ref[rows, 512:] + times(columns(x_ref, rows, dev_ref, x_group(2)), b_low, b_high),
        )
        parts = []
        for k in range(KV_HEADS):
            at = (k % 4) * 128
            key = halves[k // 4][:, at : at + 128]
            key = (key * cosine + pltpu.roll(key, 64, 1) * sine).astype(jnp.bfloat16)
            one = lax.dot_general(
                q, key, (((1,), (1,)), ((), ())), preferred_element_type=jnp.float32
            )
            parts.append(one[k * per_key : (k + 1) * per_key])
        scale = lax.rsqrt(jnp.transpose(sum_ref[rows, :])[:1] * (1.0 / width) + EPS)
        scores = jnp.concatenate(parts, axis=0) * scale * HEAD_DIM ** (-0.5)
        slot = lax.broadcasted_iota(jnp.int32, (heads, LEN), 1)
        scores = jnp.where(slot < len_ref[2 * dev_ref[3] + c], scores, -1e30)
        expo = jnp.exp(scores - jnp.max(scores, axis=1, keepdims=True))
        probs = expo / jnp.sum(expo, axis=1, keepdims=True) * scale
        mine = lax.rem(lax.broadcasted_iota(jnp.int32, (heads, LEN), 0), 2) == c
        chosen.append(jnp.where(mine, probs, 0.0).astype(jnp.bfloat16))
    probs = jnp.concatenate(chosen, axis=1)
    for i in range(4):
        at = slice(i * 1024, (i + 1) * 1024)
        pooled = jnp.dot(probs, x_ref[:, at], preferred_element_type=jnp.float32)
        out_ref[:, :, at] = pooled.astype(jnp.bfloat16).reshape(heads // 2, 2, 1024)


def attend(dev, lengths, tokens, acc, sums, far, exchange, cosine, sine):
    peers = exchange.shape[0]
    queries = pl.BlockSpec((peers, 16, HEAD_DIM), lambda i: (0, HEAD_DIM // 16, 0))
    return pl.pallas_call(
        attend_kernel,
        out_shape=jax.ShapeDtypeStruct((peers, 2, tokens.shape[1]), jnp.bfloat16),
        grid=(1,),
        in_specs=[SMEM, SMEM] + [VMEM] * 7 + [queries, VMEM, VMEM],
        out_specs=VMEM,
        compiler_params=pltpu.CompilerParams(vmem_limit_bytes=ATTEND_LIMIT),
        name="attend",
    )(dev, lengths, tokens, acc, sums, *far, exchange, cosine, sine)


def mix_kernel(x_ref, value_ref, out_w_ref, out_ref):
    peers, two, width = x_ref.shape
    pooled = x_ref[...].reshape(peers * two, width)
    values = value_ref[...].reshape(width, HEAD_DIM)
    mixed = jnp.dot(pooled, values, preferred_element_type=jnp.float32).astype(jnp.bfloat16)
    attn = jnp.dot(mixed, out_w_ref[...], preferred_element_type=jnp.float32)
    out_ref[...] = attn.astype(jnp.bfloat16).reshape(out_ref.shape)


def mix(pooled, exchange, w_out):
    peers = exchange.shape[0]
    values = pl.BlockSpec((peers, HEAD_DIM, HEAD_DIM), lambda i: (0, 0, 0))
    return pl.pallas_call(
        mix_kernel,
        out_shape=jax.ShapeDtypeStruct(pooled.shape, jnp.bfloat16),
        grid=(1,),
        in_specs=[VMEM, values, VMEM],
        out_specs=VMEM,
        compiler_params=pltpu.CompilerParams(vmem_limit_bytes=SMALL_LIMIT),
        name="mix",
    )(pooled, exchange, w_out)


def total(parts_ref):
    out = parts_ref[0].astype(jnp.float32)
    for i in range(1, parts_ref.shape[0]):
        out = out + parts_ref[i].astype(jnp.float32)
    return out


def middle_kernel(parts_ref, own_ref, gain_ref, out_ref, after_ref):
    after = own_ref[...] + total(parts_ref)
    after_ref[...] = after
    normed = (after * row_scale(after) * gain_ref[...]).astype(jnp.bfloat16)
    out_ref[...] = jnp.broadcast_to(normed[None], out_ref.shape)


def middle(parts, own_last, gain):
    return pl.pallas_call(
        middle_kernel,
        out_shape=(
            jax.ShapeDtypeStruct(parts.shape, jnp.bfloat16),
            jax.ShapeDtypeStruct(own_last.shape, jnp.float32),
        ),
        in_specs=[VMEM] * 3,
        out_specs=(VMEM, VMEM),
        compiler_params=pltpu.CompilerParams(vmem_limit_bytes=SMALL_LIMIT),
        name="middle",
    )(parts, own_last, gain)


def mlp_kernel(x_ref, gate_ref, up_ref, down_ref, out_ref):
    peers, two, width = x_ref.shape
    x = x_ref[...].reshape(peers * two, width)
    dims = (((1,), (1,)), ((), ()))
    gate = lax.dot_general(gate_ref[...], x, dims, preferred_element_type=jnp.float32)
    up = lax.dot_general(up_ref[...], x, dims, preferred_element_type=jnp.float32)
    act = jnp.transpose(gate / (1.0 + jnp.exp(-gate)) * up).astype(jnp.bfloat16)
    down = jnp.dot(act, down_ref[...], preferred_element_type=jnp.float32)
    out_ref[...] = down.astype(jnp.bfloat16).reshape(out_ref.shape)


def mlp(x, w_gate, w_up, w_down):
    return pl.pallas_call(
        mlp_kernel,
        out_shape=jax.ShapeDtypeStruct(x.shape, jnp.bfloat16),
        in_specs=[VMEM] * 4,
        out_specs=VMEM,
        compiler_params=pltpu.CompilerParams(vmem_limit_bytes=SMALL_LIMIT),
        name="mlp",
    )(x, w_gate, w_up, w_down)


def finish_kernel(parts_ref, after_ref, gain_ref, head_ref, out_ref):
    after = after_ref[...] + total(parts_ref)
    features = after * row_scale(after) * gain_ref[...]
    score = jnp.sum(features * head_ref[...], axis=1, keepdims=True)
    lane = lax.broadcasted_iota(jnp.int32, (1, 128), 1)
    tail = jnp.where(lane == 0, score[:1], jnp.where(lane == 1, score[1:], 0.0))
    peers = parts_ref.shape[0]
    for d in range(peers):
        cols = slice(d * 128, (d + 1) * 128)
        line = jnp.concatenate([features[:1, cols], features[1:, cols], tail], axis=1)
        for j in range(out_ref.shape[0] // peers):
            out_ref[j * peers + d] = line


def finish(parts, after_attn, gain, reward, devices):
    return pl.pallas_call(
        finish_kernel,
        out_shape=jax.ShapeDtypeStruct((devices, 1, 384), jnp.float32),
        in_specs=[VMEM] * 4,
        out_specs=VMEM,
        compiler_params=pltpu.CompilerParams(vmem_limit_bytes=SMALL_LIMIT),
        name="finish",
    )(parts, after_attn, gain, reward)


def remaining_candidates(judge_panel, duplicate_group_index, duplicate_groups):
    same = duplicate_group_index[:, None] == duplicate_group_index[None, :]
    top = jnp.max(jnp.where(same, judge_panel[None, :], -1e30), axis=1)
    expo = jnp.exp(judge_panel - top)
    total = jnp.sum(jnp.where(same, expo[None, :], 0.0), axis=1)
    weight_values = expo / total
    panel_member = (
        duplicate_group_index[:, None] == jnp.arange(duplicate_groups, dtype=jnp.int32)[None, :]
    ).astype(jnp.float32)
    return (weight_values, panel_member)


def layer(
    hidden,
    lengths,
    duplicate_group_index,
    attn_gain,
    w_query,
    w_key,
    w_value,
    w_out,
    mlp_gain,
    w_gate,
    w_up,
    w_down,
    final_gain,
    reward_head,
):
    judges = lax.axis_size("judge")
    devices = lax.axis_size("fsdp")
    me = lax.axis_index("fsdp")
    dev = jnp.stack([me // (NX * NZ), (me // NZ) % NX, me % NZ, me]).astype(jnp.int32)
    key_cos, key_sin = angles(jnp.arange(LEN, dtype=jnp.float32))
    tables = (
        jnp.concatenate([key_cos, key_cos], axis=1),
        jnp.concatenate([-key_sin, key_sin], axis=1),
    )
    tokens = hidden[0]
    tok_dev, width = tokens.shape
    seq_dev = tok_dev // LEN
    cands = lengths.shape[0]
    assert devices == GROUP and seq_dev == 2
    duplicate_groups = cands // 4

    row_gain = attn_gain[0].astype(jnp.float32)[:, None]
    key_rows = (w_key[0].astype(jnp.float32) * row_gain).astype(jnp.bfloat16)
    other = moved(key_rows, dy=1)
    both = jnp.concatenate([key_rows, other])
    line_x = small_ring(both[:, :512], "dx")
    line_z = small_ring(both[:, 512:], "dz")
    near_z, far_z = large_ring(*line_x, "dz")
    near_x, far_x = large_ring(*line_z, "dx")

    packed, own_last = pack_last(
        me[None], lengths, tokens, attn_gain, mlp_gain, final_gain, devices
    )
    shared = exchanged(packed, "fsdp")
    x_last = shared[:, :, :width].reshape(cands, width).astype(jnp.float32)
    gain_attn = shared[:, 0, width : width + 128].reshape(1, width).astype(jnp.float32)
    gain_final = shared[:, 0, width + 128 :].reshape(1, width).astype(jnp.float32)
    gain_mlp = shared[:, 1, width : width + 128].reshape(1, width).astype(jnp.float32)

    q_norm = (x_last * row_scale(x_last) * gain_attn).astype(jnp.bfloat16)
    q_part = jnp.dot(q_norm, w_query[0], preferred_element_type=jnp.float32)
    cosine, sine = angles((lengths - 1).astype(jnp.float32))
    q_part = rotate(q_part, cosine, sine).astype(jnp.bfloat16)
    value_rows = (w_value[0].astype(jnp.float32) * row_gain).astype(jnp.bfloat16)
    value_cols = jnp.swapaxes(value_rows.reshape(128, KV_HEADS, HEAD_DIM), 0, 1)
    value_cols = jnp.repeat(value_cols, devices // KV_HEADS, axis=0)
    q_part = jnp.pad(q_part.reshape(devices, seq_dev, HEAD_DIM), ((0, 0), (0, 14), (0, 0)))
    parcel = jnp.concatenate([value_cols, q_part], axis=1)
    both = exchanged(parcel, "fsdp")
    acc, sums, near_tokens = own_keys(dev, tokens, (*line_x, *line_z))
    acc = near_keys(dev, near_tokens, acc, (*near_z, *near_x))
    pooled = attend(
        dev,
        lengths,
        near_tokens,
        acc,
        sums,
        (*far_z, *far_x),
        both,
        *tables,
    )
    pooled = exchanged(pooled, "fsdp")
    attn = mix(pooled, both, w_out[0])
    attn = exchanged(attn, "fsdp")
    m_norm, after_attn = middle(attn, own_last, gain_mlp)
    m_norm = exchanged(m_norm, "fsdp")
    down = mlp(m_norm, w_gate[0].T, w_up[0].T, w_down[0])
    down = exchanged(down, "fsdp")

    cols = finish(down, after_attn, gain_final, reward_head, judges * devices)
    cols = exchanged(cols, ("judge", "fsdp"))
    mean = jnp.sum(cols.reshape(judges, devices, 384), axis=0) / judges
    total_cols = mean[:, :256].reshape(cands, 128)
    panel = mean[:, 256 : 256 + seq_dev].reshape(cands)
    weight_values, panel_member = remaining_candidates(
        panel, duplicate_group_index, duplicate_groups
    )
    cluster_cols = jnp.dot(
        panel_member.T, weight_values[:, None] * total_cols, precision=lax.Precision.HIGHEST
    )
    return (weight_values, cluster_cols)


def solution(mesh):
    in_specs = (
        P("judge", "fsdp", None),
        P(),
        P(),
        P("judge", "fsdp"),
        P("judge", None, "fsdp"),
        P("judge", "fsdp", None),
        P("judge", "fsdp", None),
        P("judge", "fsdp", None),
        P("judge", "fsdp"),
        P("judge", None, "fsdp"),
        P("judge", None, "fsdp"),
        P("judge", "fsdp", None),
        P("judge", "fsdp"),
        P("judge", None),
    )
    out_specs = (P(), P(None, "fsdp"))
    return jax.shard_map(layer, mesh=mesh, in_specs=in_specs, out_specs=out_specs, check_vma=False)
```

```python
import math

import jax
import jax.numpy as jnp
from jax import lax
from jax.experimental import pallas as pl
from jax.experimental.pallas import tpu as pltpu
from jax.sharding import PartitionSpec as P


KV_HEADS = 8
HEAD_DIM = 128
LEN = 512
EPS = 1e-05
ROPE_BASE = 500000.0
NY, NX, NZ = 2, 4, 4
GROUP = NY * NX * NZ


ROWS = 256
VMEM = pl.BlockSpec(memory_space=pltpu.VMEM)
SMEM = pl.BlockSpec(memory_space=pltpu.SMEM)
OWN_LIMIT = 16 << 20
SMALL_LIMIT = 12 << 20
NEAR_LIMIT = 16 << 20
ATTEND_LIMIT = 20 << 20


def place(y, x, z):
    return ((y % NY) * NX + x % NX) * NZ + z % NZ


def moved(v, dy=0, dx=0, dz=0):
    pairs = [
        (place(y, x, z), place(y + dy, x + dx, z + dz))
        for y in range(NY)
        for x in range(NX)
        for z in range(NZ)
    ]
    return lax.ppermute(v, "fsdp", pairs)


def along(v, name, step):
    return moved(v, **{name: step})


def small_ring(v, name):
    after = along(v, name, -1)
    before = along(v, name, 1)
    opposite = along(v, name, 2)
    return jnp.stack([v, after]), jnp.stack([opposite, before])


def large_ring(low, high, name):
    before_low = along(low, name, 1)
    after_high = along(high, name, -1)
    before_high = along(high, name, 1)
    after_low = along(low, name, -1)
    far = (along(before_low, name, 1), along(after_high, name, -1))
    return (after_low, after_high, before_low, before_high), far


def exchanged(x, axis):
    return lax.all_to_all(x, axis, 0, 0, tiled=True)


def row_scale(v):
    return lax.rsqrt(jnp.mean(v * v, axis=-1, keepdims=True) + EPS)


def angles(position):
    half = HEAD_DIM // 2
    freq = jnp.exp(jnp.arange(half, dtype=jnp.float32) * (-2.0 * math.log(ROPE_BASE) / HEAD_DIM))
    turned = position[..., None] * freq
    return (jnp.cos(turned), jnp.sin(turned))


def turn_tables(position):
    cosine, sine = angles(position)
    return (
        jnp.concatenate([cosine, cosine], axis=-1),
        jnp.concatenate([-sine, sine], axis=-1),
    )


def column_of(pos_ref, zo, xo, yo):
    y = lax.rem(pos_ref[0] + yo, NY)
    x = lax.rem(pos_ref[1] + xo, NX)
    z = lax.rem(pos_ref[2] + zo, NZ)
    return pl.multiple_of(((y * NX + x) * NZ + z) * 128, 128)


def pack_kernel(dev_ref, len_ref, x0_ref, x1_ref, ga_ref, gm_ref, gf_ref, out_ref, own_ref):
    width = x0_ref.shape[1]
    peers = out_ref.shape[0]
    rows = []
    for i, x_ref in enumerate((x0_ref, x1_ref)):
        slot = lax.rem(len_ref[2 * dev_ref[0] + i] - 1, 16)
        x = x_ref[...].astype(jnp.float32)
        own = lax.broadcasted_iota(jnp.int32, x.shape, 0) == slot
        rows.append(jnp.sum(jnp.where(own, x, 0.0), axis=0, keepdims=True))
    own_ref[...] = jnp.concatenate(rows, axis=0)
    gains = [g[...].astype(jnp.float32) for g in (ga_ref, gm_ref, gf_ref)]
    first = jnp.concatenate([rows[0], gains[0], gains[2]], axis=1)
    second = jnp.concatenate([rows[1], gains[1], gains[1]], axis=1)
    both = jnp.concatenate([first, second], axis=0).astype(jnp.bfloat16)
    out_ref[...] = jnp.broadcast_to(both[None], (peers, 2, width + 256))


def pack_last(dev, lengths, tokens, attn_gain, mlp_gain, final_gain, peers):
    width = tokens.shape[1]

    def row_block(i):
        return pl.BlockSpec(
            (16, width), lambda s, d, n: ((i * LEN + n[2 * d[0] + i] - 1) // 16, 0)
        )

    gain = pl.BlockSpec((1, 128), lambda s, d, n: (0, 0))
    return pl.pallas_call(
        pack_kernel,
        out_shape=(
            jax.ShapeDtypeStruct((peers, 2, width + 256), jnp.bfloat16),
            jax.ShapeDtypeStruct((2, width), jnp.float32),
        ),
        grid_spec=pltpu.PrefetchScalarGridSpec(
            num_scalar_prefetch=2,
            grid=(1,),
            in_specs=[row_block(0), row_block(1), gain, gain, gain],
            out_specs=(
                pl.BlockSpec((peers, 2, width + 256), lambda s, d, n: (0, 0, 0)),
                pl.BlockSpec((2, width), lambda s, d, n: (0, 0)),
            ),
        ),
        name="pack_last",
    )(dev, lengths, tokens, tokens, attn_gain, mlp_gain, final_gain)


def parcel_kernel(
    shared_ref, w_ref, cos_ref, sin_ref, value_ref, out_ref, mlp_ref, final_ref
):
    peers = shared_ref.shape[0]
    width = w_ref.shape[0]

    def gain(row, at):
        lines = shared_ref[:, row, at : at + 128].astype(jnp.float32)
        return jnp.concatenate([lines[d : d + 1] for d in range(peers)], axis=1)

    mlp_ref[...] = gain(1, width)
    final_ref[...] = gain(0, width + 128)
    each = peers // KV_HEADS
    for k in range(KV_HEADS):
        for h in range(k * each, (k + 1) * each):
            out_ref[h, :HEAD_DIM] = value_ref[k]
    x = shared_ref[:, :, :width].reshape(2 * peers, width).astype(jnp.float32)
    normed = (x * row_scale(x) * gain(0, width)).astype(jnp.bfloat16)
    q = jnp.dot(normed, w_ref[...], preferred_element_type=jnp.float32)
    q = (q * cos_ref[...] + pltpu.roll(q, 64, 1) * sin_ref[...]).reshape(peers, 2, HEAD_DIM)
    q = jnp.concatenate([q, jnp.zeros((peers, 14, HEAD_DIM), jnp.float32)], axis=1)
    out_ref[:, HEAD_DIM:] = q.astype(jnp.bfloat16)


def make_parcel(shared, w_query, turns, value_cols):
    peers = shared.shape[0]
    width = w_query.shape[0]
    return pl.pallas_call(
        parcel_kernel,
        out_shape=(
            jax.ShapeDtypeStruct((peers, HEAD_DIM + 16, HEAD_DIM), jnp.bfloat16),
            jax.ShapeDtypeStruct((1, width), jnp.float32),
            jax.ShapeDtypeStruct((1, width), jnp.float32),
        ),
        in_specs=[VMEM] * 5,
        out_specs=(VMEM,) * 3,
        compiler_params=pltpu.CompilerParams(vmem_limit_bytes=SMALL_LIMIT),
        name="parcel",
    )(shared, w_query, *turns, value_cols)


def columns(x_ref, rows, dev_ref, blocks):
    parts = []
    for zo, xo in blocks:
        for yo in range(NY):
            parts.append(x_ref[rows, pl.ds(column_of(dev_ref, zo, xo, yo), 128)])
    return jnp.concatenate(parts, axis=1)


def times(lhs, low, high):
    half = lhs.shape[1] // 2
    return jnp.dot(
        lhs[:, :half], low[...].reshape(half, -1), preferred_element_type=jnp.float32
    ) + jnp.dot(lhs[:, half:], high[...].reshape(half, -1), preferred_element_type=jnp.float32)


def z_group(off):
    return [(off, i) for i in range(NX)]


def x_group(off):
    return [(i, off) for i in range(NZ)]


def own_keys_kernel(dev_ref, hbm_ref, a_low, a_high, b_low, b_high, out_ref, sum_ref, x_ref, sems):
    steps = hbm_ref.shape[0] // ROWS
    copies = []
    for i in range(steps):
        rows = pl.ds(i * ROWS, ROWS)
        copies.append(pltpu.make_async_copy(hbm_ref.at[rows], x_ref.at[rows], sems.at[i]))
        copies[i].start()
    for i in range(steps):
        rows = pl.ds(i * ROWS, ROWS)
        copies[i].wait()
        out_ref[rows, :512] = times(columns(x_ref, rows, dev_ref, z_group(0)), a_low, a_high)
        out_ref[rows, 512:] = times(columns(x_ref, rows, dev_ref, x_group(0)), b_low, b_high)
        x = x_ref[rows, :].astype(jnp.float32)
        sum_ref[rows, :] = jnp.broadcast_to(jnp.sum(x * x, axis=1, keepdims=True), (ROWS, 128))


def near_keys_kernel(dev_ref, x_ref, acc_ref, a1l, a1h, a3l, a3h, b1l, b1h, b3l, b3h, out_ref):
    def step(i, carry):
        rows = pl.ds(pl.multiple_of(i * ROWS, ROWS), ROWS)
        first = acc_ref[rows, :512]
        first += times(columns(x_ref, rows, dev_ref, z_group(1)), a1l, a1h)
        first += times(columns(x_ref, rows, dev_ref, z_group(3)), a3l, a3h)
        out_ref[rows, :512] = first
        second = acc_ref[rows, 512:]
        second += times(columns(x_ref, rows, dev_ref, x_group(1)), b1l, b1h)
        second += times(columns(x_ref, rows, dev_ref, x_group(3)), b3l, b3h)
        out_ref[rows, 512:] = second
        return carry

    lax.fori_loop(0, x_ref.shape[0] // ROWS, step, 0)


def own_keys(dev, tokens, parts):
    rows = tokens.shape[0]
    return pl.pallas_call(
        own_keys_kernel,
        out_shape=(
            jax.ShapeDtypeStruct((rows, 1024), jnp.float32),
            jax.ShapeDtypeStruct((rows, 128), jnp.float32),
            jax.ShapeDtypeStruct(tokens.shape, tokens.dtype),
        ),
        in_specs=[SMEM, pl.BlockSpec(memory_space=pltpu.HBM)] + [VMEM] * 4,
        out_specs=(VMEM, VMEM, VMEM),
        scratch_shapes=[pltpu.SemaphoreType.DMA((rows // ROWS,))],
        compiler_params=pltpu.CompilerParams(vmem_limit_bytes=OWN_LIMIT),
        name="own_keys",
    )(dev, pltpu.with_memory_space_constraint(tokens, pltpu.HBM), *parts)


def near_keys(dev, tokens, acc, parts):
    return pl.pallas_call(
        near_keys_kernel,
        out_shape=jax.ShapeDtypeStruct(acc.shape, jnp.float32),
        in_specs=[SMEM] + [VMEM] * 10,
        out_specs=VMEM,
        input_output_aliases={2: 0},
        compiler_params=pltpu.CompilerParams(vmem_limit_bytes=NEAR_LIMIT),
        name="near_keys",
    )(dev, tokens, acc, *parts)


def attend_kernel(
    dev_ref,
    len_ref,
    x_ref,
    acc_ref,
    sum_ref,
    a_low,
    a_high,
    b_low,
    b_high,
    q_ref,
    cos_ref,
    sin_ref,
    out_ref,
):
    width = x_ref.shape[1]
    heads = q_ref.shape[0] * 2
    per_key = heads // KV_HEADS
    cosine = cos_ref[...]
    sine = sin_ref[...]
    q = q_ref[:, :2, :].reshape(heads, HEAD_DIM)
    chosen = []
    for c in range(2):
        rows = pl.ds(c * LEN, LEN)
        halves = (
            acc_ref[rows, :512] + times(columns(x_ref, rows, dev_ref, z_group(2)), a_low, a_high),
            acc_ref[rows, 512:] + times(columns(x_ref, rows, dev_ref, x_group(2)), b_low, b_high),
        )
        parts = []
        for k in range(KV_HEADS):
            at = (k % 4) * 128
            key = halves[k // 4][:, at : at + 128]
            key = (key * cosine + pltpu.roll(key, 64, 1) * sine).astype(jnp.bfloat16)
            one = lax.dot_general(
                q, key, (((1,), (1,)), ((), ())), preferred_element_type=jnp.float32
            )
            parts.append(one[k * per_key : (k + 1) * per_key])
        scale = lax.rsqrt(jnp.transpose(sum_ref[rows, :])[:1] * (1.0 / width) + EPS)
        scores = jnp.concatenate(parts, axis=0) * scale * HEAD_DIM ** (-0.5)
        slot = lax.broadcasted_iota(jnp.int32, (heads, LEN), 1)
        scores = jnp.where(slot < len_ref[2 * dev_ref[3] + c], scores, -1e30)
        expo = jnp.exp(scores - jnp.max(scores, axis=1, keepdims=True))
        probs = expo / jnp.sum(expo, axis=1, keepdims=True) * scale
        mine = lax.rem(lax.broadcasted_iota(jnp.int32, (heads, LEN), 0), 2) == c
        chosen.append(jnp.where(mine, probs, 0.0).astype(jnp.bfloat16))
    probs = jnp.concatenate(chosen, axis=1)
    for i in range(4):
        at = slice(i * 1024, (i + 1) * 1024)
        pooled = jnp.dot(probs, x_ref[:, at], preferred_element_type=jnp.float32)
        out_ref[:, :, at] = pooled.astype(jnp.bfloat16).reshape(heads // 2, 2, 1024)


def attend(dev, lengths, tokens, acc, sums, far, exchange, cosine, sine):
    peers = exchange.shape[0]
    queries = pl.BlockSpec((peers, 16, HEAD_DIM), lambda i: (0, HEAD_DIM // 16, 0))
    return pl.pallas_call(
        attend_kernel,
        out_shape=jax.ShapeDtypeStruct((peers, 2, tokens.shape[1]), jnp.bfloat16),
        grid=(1,),
        in_specs=[SMEM, SMEM] + [VMEM] * 7 + [queries, VMEM, VMEM],
        out_specs=VMEM,
        compiler_params=pltpu.CompilerParams(vmem_limit_bytes=ATTEND_LIMIT),
        name="attend",
    )(dev, lengths, tokens, acc, sums, *far, exchange, cosine, sine)


def mix_kernel(x_ref, value_ref, out_w_ref, out_ref):
    peers, two, width = x_ref.shape
    pooled = x_ref[...].reshape(peers * two, width)
    values = value_ref[...].reshape(width, HEAD_DIM)
    mixed = jnp.dot(pooled, values, preferred_element_type=jnp.float32).astype(jnp.bfloat16)
    attn = jnp.dot(mixed, out_w_ref[...], preferred_element_type=jnp.float32)
    out_ref[...] = attn.astype(jnp.bfloat16).reshape(out_ref.shape)


def mix(pooled, exchange, w_out):
    peers = exchange.shape[0]
    values = pl.BlockSpec((peers, HEAD_DIM, HEAD_DIM), lambda i: (0, 0, 0))
    return pl.pallas_call(
        mix_kernel,
        out_shape=jax.ShapeDtypeStruct(pooled.shape, jnp.bfloat16),
        grid=(1,),
        in_specs=[VMEM, values, VMEM],
        out_specs=VMEM,
        compiler_params=pltpu.CompilerParams(vmem_limit_bytes=SMALL_LIMIT),
        name="mix",
    )(pooled, exchange, w_out)


def total(parts_ref):
    out = parts_ref[0].astype(jnp.float32)
    for i in range(1, parts_ref.shape[0]):
        out = out + parts_ref[i].astype(jnp.float32)
    return out


def middle_kernel(parts_ref, own_ref, gain_ref, out_ref, after_ref):
    after = own_ref[...] + total(parts_ref)
    after_ref[...] = after
    normed = (after * row_scale(after) * gain_ref[...]).astype(jnp.bfloat16)
    out_ref[...] = jnp.broadcast_to(normed[None], out_ref.shape)


def middle(parts, own_last, gain):
    return pl.pallas_call(
        middle_kernel,
        out_shape=(
            jax.ShapeDtypeStruct(parts.shape, jnp.bfloat16),
            jax.ShapeDtypeStruct(own_last.shape, jnp.float32),
        ),
        in_specs=[VMEM] * 3,
        out_specs=(VMEM, VMEM),
        compiler_params=pltpu.CompilerParams(vmem_limit_bytes=SMALL_LIMIT),
        name="middle",
    )(parts, own_last, gain)


def mlp_kernel(x_ref, gate_ref, up_ref, down_ref, out_ref):
    peers, two, width = x_ref.shape
    x = x_ref[...].reshape(peers * two, width)
    dims = (((1,), (1,)), ((), ()))
    gate = lax.dot_general(gate_ref[...], x, dims, preferred_element_type=jnp.float32)
    up = lax.dot_general(up_ref[...], x, dims, preferred_element_type=jnp.float32)
    act = jnp.transpose(gate / (1.0 + jnp.exp(-gate)) * up).astype(jnp.bfloat16)
    down = jnp.dot(act, down_ref[...], preferred_element_type=jnp.float32)
    out_ref[...] = down.astype(jnp.bfloat16).reshape(out_ref.shape)


def mlp(x, w_gate, w_up, w_down):
    return pl.pallas_call(
        mlp_kernel,
        out_shape=jax.ShapeDtypeStruct(x.shape, jnp.bfloat16),
        in_specs=[VMEM] * 4,
        out_specs=VMEM,
        compiler_params=pltpu.CompilerParams(vmem_limit_bytes=SMALL_LIMIT),
        name="mlp",
    )(x, w_gate, w_up, w_down)


def finish_kernel(parts_ref, after_ref, gain_ref, head_ref, out_ref):
    after = after_ref[...] + total(parts_ref)
    features = after * row_scale(after) * gain_ref[...]
    score = jnp.sum(features * head_ref[...], axis=1, keepdims=True)
    lane = lax.broadcasted_iota(jnp.int32, (1, 128), 1)
    tail = jnp.where(lane == 0, score[:1], jnp.where(lane == 1, score[1:], 0.0))
    peers = parts_ref.shape[0]
    for d in range(peers):
        cols = slice(d * 128, (d + 1) * 128)
        line = jnp.concatenate([features[:1, cols], features[1:, cols], tail], axis=1)
        for j in range(out_ref.shape[0] // peers):
            out_ref[j * peers + d] = line


def finish(parts, after_attn, gain, reward, devices):
    return pl.pallas_call(
        finish_kernel,
        out_shape=jax.ShapeDtypeStruct((devices, 1, 384), jnp.float32),
        in_specs=[VMEM] * 4,
        out_specs=VMEM,
        compiler_params=pltpu.CompilerParams(vmem_limit_bytes=SMALL_LIMIT),
        name="finish",
    )(parts, after_attn, gain, reward)


def remaining_candidates(judge_panel, duplicate_group_index, duplicate_groups):
    same = duplicate_group_index[:, None] == duplicate_group_index[None, :]
    top = jnp.max(jnp.where(same, judge_panel[None, :], -1e30), axis=1)
    expo = jnp.exp(judge_panel - top)
    total = jnp.sum(jnp.where(same, expo[None, :], 0.0), axis=1)
    weight_values = expo / total
    panel_member = (
        duplicate_group_index[:, None] == jnp.arange(duplicate_groups, dtype=jnp.int32)[None, :]
    ).astype(jnp.float32)
    return (weight_values, panel_member)


def layer(
    hidden,
    lengths,
    duplicate_group_index,
    attn_gain,
    w_query,
    w_key,
    w_value,
    w_out,
    mlp_gain,
    w_gate,
    w_up,
    w_down,
    final_gain,
    reward_head,
):
    judges = lax.axis_size("judge")
    devices = lax.axis_size("fsdp")
    me = lax.axis_index("fsdp")
    dev = jnp.stack([me // (NX * NZ), (me // NZ) % NX, me % NZ, me]).astype(jnp.int32)
    turns = turn_tables((lengths - 1).astype(jnp.float32))
    tokens = hidden[0]
    tok_dev, _ = tokens.shape
    seq_dev = tok_dev // LEN
    cands = lengths.shape[0]
    assert devices == GROUP and seq_dev == 2
    duplicate_groups = cands // 4

    row_gain = attn_gain[0].astype(jnp.float32)[:, None]
    other = moved(w_key[0], dy=1)
    other_gain = moved(attn_gain[0], dy=1).astype(jnp.float32)[:, None]
    both = jnp.concatenate(
        [
            (w_key[0].astype(jnp.float32) * row_gain).astype(jnp.bfloat16),
            (other.astype(jnp.float32) * other_gain).astype(jnp.bfloat16),
        ]
    )
    line_x = small_ring(both[:, :512], "dx")
    line_z = small_ring(both[:, 512:], "dz")
    near_z, far_z = large_ring(*line_x, "dz")
    near_x, far_x = large_ring(*line_z, "dx")

    tables = turn_tables(jnp.arange(LEN, dtype=jnp.float32))

    packed, own_last = pack_last(
        me[None], lengths, tokens, attn_gain, mlp_gain, final_gain, devices
    )
    shared = exchanged(packed, "fsdp")
    value_rows = (w_value[0].astype(jnp.float32) * row_gain).astype(jnp.bfloat16)
    value_cols = jnp.swapaxes(value_rows.reshape(128, KV_HEADS, HEAD_DIM), 0, 1)
    parcel, gain_mlp, gain_final = make_parcel(shared, w_query[0], turns, value_cols)
    both = exchanged(parcel, "fsdp")

    acc, sums, near_tokens = own_keys(dev, tokens, (*line_x, *line_z))
    acc = near_keys(dev, near_tokens, acc, (*near_z, *near_x))
    pooled = attend(
        dev,
        lengths,
        near_tokens,
        acc,
        sums,
        (*far_z, *far_x),
        both,
        *tables,
    )
    pooled = exchanged(pooled, "fsdp")
    attn = mix(pooled, both, w_out[0])
    attn = exchanged(attn, "fsdp")
    m_norm, after_attn = middle(attn, own_last, gain_mlp)
    m_norm = exchanged(m_norm, "fsdp")
    down = mlp(m_norm, w_gate[0].T, w_up[0].T, w_down[0])
    down = exchanged(down, "fsdp")

    cols = finish(down, after_attn, gain_final, reward_head, judges * devices)
    cols = exchanged(cols, ("judge", "fsdp"))
    mean = jnp.sum(cols.reshape(judges, devices, 384), axis=0) / judges
    total_cols = mean[:, :256].reshape(cands, 128)
    panel = mean[:, 256 : 256 + seq_dev].reshape(cands)
    weight_values, panel_member = remaining_candidates(
        panel, duplicate_group_index, duplicate_groups
    )
    cluster_cols = jnp.dot(
        panel_member.T, weight_values[:, None] * total_cols, precision=lax.Precision.HIGHEST
    )
    return (weight_values, cluster_cols)


def solution(mesh):
    in_specs = (
        P("judge", "fsdp", None),
        P(),
        P(),
        P("judge", "fsdp"),
        P("judge", None, "fsdp"),
        P("judge", "fsdp", None),
        P("judge", "fsdp", None),
        P("judge", "fsdp", None),
        P("judge", "fsdp"),
        P("judge", None, "fsdp"),
        P("judge", None, "fsdp"),
        P("judge", "fsdp", None),
        P("judge", "fsdp"),
        P("judge", None),
    )
    out_specs = (P(), P(None, "fsdp"))
    return jax.shard_map(layer, mesh=mesh, in_specs=in_specs, out_specs=out_specs, check_vma=False)
```

```python
import functools
import math

import jax
import jax.numpy as jnp
from jax import lax
from jax.experimental import pallas as pl
from jax.experimental.pallas import tpu as pltpu
from jax.sharding import PartitionSpec as P


KV_HEADS = 8
HEAD_DIM = 128
LEN = 512
EPS = 1e-05
ROPE_BASE = 500000.0
NY, NX, NZ = 2, 4, 4
GROUP = NY * NX * NZ


ROWS = 256
VMEM = pl.BlockSpec(memory_space=pltpu.VMEM)
SMEM = pl.BlockSpec(memory_space=pltpu.SMEM)
OWN_LIMIT = 16 << 20
SMALL_LIMIT = 12 << 20
NEAR_LIMIT = 16 << 20
ATTEND_LIMIT = 20 << 20


def place(y, x, z):
    return ((y % NY) * NX + x % NX) * NZ + z % NZ


def moved(v, dy=0, dx=0, dz=0):
    pairs = [
        (place(y, x, z), place(y + dy, x + dx, z + dz))
        for y in range(NY)
        for x in range(NX)
        for z in range(NZ)
    ]
    return lax.ppermute(v, "fsdp", pairs)


def along(v, name, step):
    return moved(v, **{name: step})


def small_ring(v, name):
    after = along(v, name, -1)
    before = along(v, name, 1)
    opposite = along(v, name, 2)
    return jnp.stack([v, after]), jnp.stack([opposite, before])


def large_ring(low, high, name):
    before_low = along(low, name, 1)
    after_high = along(high, name, -1)
    before_high = along(high, name, 1)
    after_low = along(low, name, -1)
    far = (along(before_low, name, 1), along(after_high, name, -1))
    return (after_low, after_high, before_low, before_high), far


def exchanged(x, axis):
    return lax.all_to_all(x, axis, 0, 0, tiled=True)


def row_scale(v):
    return lax.rsqrt(jnp.mean(v * v, axis=-1, keepdims=True) + EPS)


def angles(position):
    half = HEAD_DIM // 2
    freq = jnp.exp(jnp.arange(half, dtype=jnp.float32) * (-2.0 * math.log(ROPE_BASE) / HEAD_DIM))
    turned = position[..., None] * freq
    return (jnp.cos(turned), jnp.sin(turned))


def turn_tables(position):
    cosine, sine = angles(position)
    return (
        jnp.concatenate([cosine, cosine], axis=-1),
        jnp.concatenate([-sine, sine], axis=-1),
    )


def column_of(pos_ref, zo, xo, yo):
    y = lax.rem(pos_ref[0] + yo, NY)
    x = lax.rem(pos_ref[1] + xo, NX)
    z = lax.rem(pos_ref[2] + zo, NZ)
    return pl.multiple_of(((y * NX + x) * NZ + z) * 128, 128)


def pack_kernel(dev_ref, len_ref, x0_ref, x1_ref, ga_ref, gm_ref, gf_ref, out_ref, own_ref):
    width = x0_ref.shape[1]
    peers = out_ref.shape[0]
    rows = []
    for i, x_ref in enumerate((x0_ref, x1_ref)):
        slot = lax.rem(len_ref[2 * dev_ref[0] + i] - 1, 16)
        x = x_ref[...].astype(jnp.float32)
        own = lax.broadcasted_iota(jnp.int32, x.shape, 0) == slot
        rows.append(jnp.sum(jnp.where(own, x, 0.0), axis=0, keepdims=True))
    own_ref[...] = jnp.concatenate(rows, axis=0)
    gains = [g[...].astype(jnp.float32) for g in (ga_ref, gm_ref, gf_ref)]
    first = jnp.concatenate([rows[0], gains[0], gains[2]], axis=1)
    second = jnp.concatenate([rows[1], gains[1], gains[1]], axis=1)
    both = jnp.concatenate([first, second], axis=0).astype(jnp.bfloat16)
    out_ref[...] = jnp.broadcast_to(both[None], (peers, 2, width + 256))


def pack_last(dev, lengths, tokens, attn_gain, mlp_gain, final_gain, peers):
    width = tokens.shape[1]

    def row_block(i):
        return pl.BlockSpec(
            (16, width), lambda s, d, n: ((i * LEN + n[2 * d[0] + i] - 1) // 16, 0)
        )

    gain = pl.BlockSpec((1, 128), lambda s, d, n: (0, 0))
    return pl.pallas_call(
        pack_kernel,
        out_shape=(
            jax.ShapeDtypeStruct((peers, 2, width + 256), jnp.bfloat16),
            jax.ShapeDtypeStruct((2, width), jnp.float32),
        ),
        grid_spec=pltpu.PrefetchScalarGridSpec(
            num_scalar_prefetch=2,
            grid=(1,),
            in_specs=[row_block(0), row_block(1), gain, gain, gain],
            out_specs=(
                pl.BlockSpec((peers, 2, width + 256), lambda s, d, n: (0, 0, 0)),
                pl.BlockSpec((2, width), lambda s, d, n: (0, 0)),
            ),
        ),
        name="pack_last",
    )(dev, lengths, tokens, tokens, attn_gain, mlp_gain, final_gain)


def parcel_kernel(
    shared_ref, w_ref, cos_ref, sin_ref, value_ref, out_ref, mlp_ref, final_ref
):
    peers = shared_ref.shape[0]
    width = w_ref.shape[0]

    def gain(row, at):
        lines = shared_ref[:, row, at : at + 128].astype(jnp.float32)
        return jnp.concatenate([lines[d : d + 1] for d in range(peers)], axis=1)

    mlp_ref[...] = gain(1, width)
    final_ref[...] = gain(0, width + 128)
    each = peers // KV_HEADS
    for k in range(KV_HEADS):
        for h in range(k * each, (k + 1) * each):
            out_ref[h, :HEAD_DIM] = value_ref[k]
    x = shared_ref[:, :, :width].reshape(2 * peers, width).astype(jnp.float32)
    normed = (x * row_scale(x) * gain(0, width)).astype(jnp.bfloat16)
    q = jnp.dot(normed, w_ref[...], preferred_element_type=jnp.float32)
    q = (q * cos_ref[...] + pltpu.roll(q, 64, 1) * sin_ref[...]).reshape(peers, 2, HEAD_DIM)
    q = jnp.concatenate([q, jnp.zeros((peers, 14, HEAD_DIM), jnp.float32)], axis=1)
    out_ref[:, HEAD_DIM:] = q.astype(jnp.bfloat16)


def make_parcel(shared, w_query, turns, value_cols):
    peers = shared.shape[0]
    width = w_query.shape[0]
    return pl.pallas_call(
        parcel_kernel,
        out_shape=(
            jax.ShapeDtypeStruct((peers, HEAD_DIM + 16, HEAD_DIM), jnp.bfloat16),
            jax.ShapeDtypeStruct((1, width), jnp.float32),
            jax.ShapeDtypeStruct((1, width), jnp.float32),
        ),
        in_specs=[VMEM] * 5,
        out_specs=(VMEM,) * 3,
        compiler_params=pltpu.CompilerParams(vmem_limit_bytes=SMALL_LIMIT),
        name="parcel",
    )(shared, w_query, *turns, value_cols)


def columns(x_ref, rows, dev_ref, blocks):
    parts = []
    for zo, xo in blocks:
        for yo in range(NY):
            parts.append(x_ref[rows, pl.ds(column_of(dev_ref, zo, xo, yo), 128)])
    return jnp.concatenate(parts, axis=1)


def times(lhs, low, high):
    half = lhs.shape[1] // 2
    return jnp.dot(
        lhs[:, :half], low[...].reshape(half, -1), preferred_element_type=jnp.float32
    ) + jnp.dot(lhs[:, half:], high[...].reshape(half, -1), preferred_element_type=jnp.float32)


def z_group(off):
    return [(off, i) for i in range(NX)]


def x_group(off):
    return [(i, off) for i in range(NZ)]


def own_keys_kernel(dev_ref, hbm_ref, a_low, a_high, b_low, b_high, out_ref, sum_ref, x_ref, sems):
    steps = hbm_ref.shape[0] // ROWS
    copies = []
    for i in range(steps):
        rows = pl.ds(i * ROWS, ROWS)
        copies.append(pltpu.make_async_copy(hbm_ref.at[rows], x_ref.at[rows], sems.at[i]))
        copies[i].start()
    for i in range(steps):
        rows = pl.ds(i * ROWS, ROWS)
        copies[i].wait()
        out_ref[rows, :512] = times(columns(x_ref, rows, dev_ref, z_group(0)), a_low, a_high)
        out_ref[rows, 512:] = times(columns(x_ref, rows, dev_ref, x_group(0)), b_low, b_high)
        x = x_ref[rows, :].astype(jnp.float32)
        sum_ref[rows, :] = jnp.broadcast_to(jnp.sum(x * x, axis=1, keepdims=True), (ROWS, 128))


def more_keys_kernel(parts, dev_ref, x_ref, acc_ref, *refs):
    out_ref = refs[-1]

    def step(i, carry):
        rows = pl.ds(pl.multiple_of(i * ROWS, ROWS), ROWS)
        for at, group in ((0, z_group), (512, x_group)):
            cols = slice(at, at + 512)
            total = acc_ref[rows, cols]
            for (side, off, half), w_ref in zip(parts, refs):
                if side == at:
                    lhs = columns(x_ref, rows, dev_ref, group(off)[2 * half : 2 * half + 2])
                    total += jnp.dot(
                        lhs, w_ref[...].reshape(512, -1), preferred_element_type=jnp.float32
                    )
            out_ref[rows, cols] = total
        return carry

    lax.fori_loop(0, x_ref.shape[0] // ROWS, step, 0)


def own_keys(dev, tokens, parts):
    rows = tokens.shape[0]
    return pl.pallas_call(
        own_keys_kernel,
        out_shape=(
            jax.ShapeDtypeStruct((rows, 1024), jnp.float32),
            jax.ShapeDtypeStruct((rows, 128), jnp.float32),
            jax.ShapeDtypeStruct(tokens.shape, tokens.dtype),
        ),
        in_specs=[SMEM, pl.BlockSpec(memory_space=pltpu.HBM)] + [VMEM] * 4,
        out_specs=(VMEM, VMEM, VMEM),
        scratch_shapes=[pltpu.SemaphoreType.DMA((rows // ROWS,))],
        compiler_params=pltpu.CompilerParams(vmem_limit_bytes=OWN_LIMIT),
        name="own_keys",
    )(dev, pltpu.with_memory_space_constraint(tokens, pltpu.HBM), *parts)


def more_keys(dev, tokens, acc, parts, arrays):
    return pl.pallas_call(
        functools.partial(more_keys_kernel, parts),
        out_shape=jax.ShapeDtypeStruct(acc.shape, jnp.float32),
        in_specs=[SMEM] + [VMEM] * (2 + len(arrays)),
        out_specs=VMEM,
        input_output_aliases={2: 0},
        compiler_params=pltpu.CompilerParams(vmem_limit_bytes=NEAR_LIMIT),
    )(dev, tokens, acc, *arrays)


def attend_kernel(
    dev_ref,
    len_ref,
    x_ref,
    acc_ref,
    sum_ref,
    a_low,
    a_high,
    q_ref,
    cos_ref,
    sin_ref,
    out_ref,
):
    width = x_ref.shape[1]
    heads = q_ref.shape[0] * 2
    per_key = heads // KV_HEADS
    cosine = cos_ref[...]
    sine = sin_ref[...]
    q = q_ref[:, :2, :].reshape(heads, HEAD_DIM)
    chosen = []
    for c in range(2):
        rows = pl.ds(c * LEN, LEN)
        halves = (
            acc_ref[rows, :512] + times(columns(x_ref, rows, dev_ref, z_group(2)), a_low, a_high),
            acc_ref[rows, 512:],
        )
        parts = []
        for k in range(KV_HEADS):
            at = (k % 4) * 128
            key = halves[k // 4][:, at : at + 128]
            key = (key * cosine + pltpu.roll(key, 64, 1) * sine).astype(jnp.bfloat16)
            one = lax.dot_general(
                q, key, (((1,), (1,)), ((), ())), preferred_element_type=jnp.float32
            )
            parts.append(one[k * per_key : (k + 1) * per_key])
        scale = lax.rsqrt(jnp.transpose(sum_ref[rows, :])[:1] * (1.0 / width) + EPS)
        scores = jnp.concatenate(parts, axis=0) * scale * HEAD_DIM ** (-0.5)
        slot = lax.broadcasted_iota(jnp.int32, (heads, LEN), 1)
        scores = jnp.where(slot < len_ref[2 * dev_ref[3] + c], scores, -1e30)
        expo = jnp.exp(scores - jnp.max(scores, axis=1, keepdims=True))
        probs = expo / jnp.sum(expo, axis=1, keepdims=True) * scale
        mine = lax.rem(lax.broadcasted_iota(jnp.int32, (heads, LEN), 0), 2) == c
        chosen.append(jnp.where(mine, probs, 0.0).astype(jnp.bfloat16))
    probs = jnp.concatenate(chosen, axis=1)
    for i in range(4):
        at = slice(i * 1024, (i + 1) * 1024)
        pooled = jnp.dot(probs, x_ref[:, at], preferred_element_type=jnp.float32)
        out_ref[:, :, at] = pooled.astype(jnp.bfloat16).reshape(heads // 2, 2, 1024)


def attend(dev, lengths, tokens, acc, sums, far, exchange, cosine, sine):
    peers = exchange.shape[0]
    queries = pl.BlockSpec((peers, 16, HEAD_DIM), lambda i: (0, HEAD_DIM // 16, 0))
    return pl.pallas_call(
        attend_kernel,
        out_shape=jax.ShapeDtypeStruct((peers, 2, tokens.shape[1]), jnp.bfloat16),
        grid=(1,),
        in_specs=[SMEM, SMEM] + [VMEM] * 5 + [queries, VMEM, VMEM],
        out_specs=VMEM,
        compiler_params=pltpu.CompilerParams(vmem_limit_bytes=ATTEND_LIMIT),
        name="attend",
    )(dev, lengths, tokens, acc, sums, *far, exchange, cosine, sine)


def mix_kernel(x_ref, value_ref, out_w_ref, out_ref):
    peers, two, width = x_ref.shape
    pooled = x_ref[...].reshape(peers * two, width)
    values = value_ref[...].reshape(width, HEAD_DIM)
    mixed = jnp.dot(pooled, values, preferred_element_type=jnp.float32).astype(jnp.bfloat16)
    attn = jnp.dot(mixed, out_w_ref[...], preferred_element_type=jnp.float32)
    out_ref[...] = attn.astype(jnp.bfloat16).reshape(out_ref.shape)


def mix(pooled, exchange, w_out):
    peers = exchange.shape[0]
    values = pl.BlockSpec((peers, HEAD_DIM, HEAD_DIM), lambda i: (0, 0, 0))
    return pl.pallas_call(
        mix_kernel,
        out_shape=jax.ShapeDtypeStruct(pooled.shape, jnp.bfloat16),
        grid=(1,),
        in_specs=[VMEM, values, VMEM],
        out_specs=VMEM,
        compiler_params=pltpu.CompilerParams(vmem_limit_bytes=SMALL_LIMIT),
        name="mix",
    )(pooled, exchange, w_out)


def total(parts_ref):
    out = parts_ref[0].astype(jnp.float32)
    for i in range(1, parts_ref.shape[0]):
        out = out + parts_ref[i].astype(jnp.float32)
    return out


def middle_kernel(parts_ref, own_ref, gain_ref, out_ref, after_ref):
    after = own_ref[...] + total(parts_ref)
    after_ref[...] = after
    normed = (after * row_scale(after) * gain_ref[...]).astype(jnp.bfloat16)
    out_ref[...] = jnp.broadcast_to(normed[None], out_ref.shape)


def middle(parts, own_last, gain):
    return pl.pallas_call(
        middle_kernel,
        out_shape=(
            jax.ShapeDtypeStruct(parts.shape, jnp.bfloat16),
            jax.ShapeDtypeStruct(own_last.shape, jnp.float32),
        ),
        in_specs=[VMEM] * 3,
        out_specs=(VMEM, VMEM),
        compiler_params=pltpu.CompilerParams(vmem_limit_bytes=SMALL_LIMIT),
        name="middle",
    )(parts, own_last, gain)


def mlp_kernel(x_ref, gate_ref, up_ref, down_ref, out_ref):
    peers, two, width = x_ref.shape
    x = x_ref[...].reshape(peers * two, width)
    dims = (((1,), (1,)), ((), ()))
    gate = lax.dot_general(gate_ref[...], x, dims, preferred_element_type=jnp.float32)
    up = lax.dot_general(up_ref[...], x, dims, preferred_element_type=jnp.float32)
    act = jnp.transpose(gate / (1.0 + jnp.exp(-gate)) * up).astype(jnp.bfloat16)
    down = jnp.dot(act, down_ref[...], preferred_element_type=jnp.float32)
    out_ref[...] = down.astype(jnp.bfloat16).reshape(out_ref.shape)


def mlp(x, w_gate, w_up, w_down):
    return pl.pallas_call(
        mlp_kernel,
        out_shape=jax.ShapeDtypeStruct(x.shape, jnp.bfloat16),
        in_specs=[VMEM] * 4,
        out_specs=VMEM,
        compiler_params=pltpu.CompilerParams(vmem_limit_bytes=SMALL_LIMIT),
        name="mlp",
    )(x, w_gate, w_up, w_down)


def finish_kernel(parts_ref, after_ref, gain_ref, head_ref, out_ref):
    after = after_ref[...] + total(parts_ref)
    features = after * row_scale(after) * gain_ref[...]
    score = jnp.sum(features * head_ref[...], axis=1, keepdims=True)
    lane = lax.broadcasted_iota(jnp.int32, (1, 128), 1)
    tail = jnp.where(lane == 0, score[:1], jnp.where(lane == 1, score[1:], 0.0))
    peers = parts_ref.shape[0]
    for d in range(peers):
        cols = slice(d * 128, (d + 1) * 128)
        line = jnp.concatenate([features[:1, cols], features[1:, cols], tail], axis=1)
        for j in range(out_ref.shape[0] // peers):
            out_ref[j * peers + d] = line


def finish(parts, after_attn, gain, reward, devices):
    return pl.pallas_call(
        finish_kernel,
        out_shape=jax.ShapeDtypeStruct((devices, 1, 384), jnp.float32),
        in_specs=[VMEM] * 4,
        out_specs=VMEM,
        compiler_params=pltpu.CompilerParams(vmem_limit_bytes=SMALL_LIMIT),
        name="finish",
    )(parts, after_attn, gain, reward)


def remaining_candidates(judge_panel, duplicate_group_index, duplicate_groups):
    same = duplicate_group_index[:, None] == duplicate_group_index[None, :]
    top = jnp.max(jnp.where(same, judge_panel[None, :], -1e30), axis=1)
    expo = jnp.exp(judge_panel - top)
    total = jnp.sum(jnp.where(same, expo[None, :], 0.0), axis=1)
    weight_values = expo / total
    panel_member = (
        duplicate_group_index[:, None] == jnp.arange(duplicate_groups, dtype=jnp.int32)[None, :]
    ).astype(jnp.float32)
    return (weight_values, panel_member)


def layer(
    hidden,
    lengths,
    duplicate_group_index,
    attn_gain,
    w_query,
    w_key,
    w_value,
    w_out,
    mlp_gain,
    w_gate,
    w_up,
    w_down,
    final_gain,
    reward_head,
):
    judges = lax.axis_size("judge")
    devices = lax.axis_size("fsdp")
    me = lax.axis_index("fsdp")
    dev = jnp.stack([me // (NX * NZ), (me // NZ) % NX, me % NZ, me]).astype(jnp.int32)
    turns = turn_tables((lengths - 1).astype(jnp.float32))
    tokens = hidden[0]
    tok_dev, _ = tokens.shape
    seq_dev = tok_dev // LEN
    cands = lengths.shape[0]
    assert devices == GROUP and seq_dev == 2
    duplicate_groups = cands // 4

    row_gain = attn_gain[0].astype(jnp.float32)[:, None]
    other = moved(w_key[0], dy=1)
    other_gain = moved(attn_gain[0], dy=1).astype(jnp.float32)[:, None]
    both = jnp.concatenate(
        [
            (w_key[0].astype(jnp.float32) * row_gain).astype(jnp.bfloat16),
            (other.astype(jnp.float32) * other_gain).astype(jnp.bfloat16),
        ]
    )
    line_x = small_ring(both[:, :512], "dx")
    line_z = small_ring(both[:, 512:], "dz")
    near_z, far_z = large_ring(*line_x, "dz")
    near_x, far_x = large_ring(*line_z, "dx")

    tables = turn_tables(jnp.arange(LEN, dtype=jnp.float32))

    packed, own_last = pack_last(
        me[None], lengths, tokens, attn_gain, mlp_gain, final_gain, devices
    )
    shared = exchanged(packed, "fsdp")
    value_rows = (w_value[0].astype(jnp.float32) * row_gain).astype(jnp.bfloat16)
    value_cols = jnp.swapaxes(value_rows.reshape(128, KV_HEADS, HEAD_DIM), 0, 1)
    parcel, gain_mlp, gain_final = make_parcel(shared, w_query[0], turns, value_cols)
    both = exchanged(parcel, "fsdp")

    acc, sums, near_tokens = own_keys(dev, tokens, (*line_x, *line_z))
    (a1l, a1h, a3l, a3h), (b1l, b1h, b3l, b3h) = near_z, near_x
    first = ((0, 1, 1), (0, 3, 0), (512, 1, 1), (512, 3, 0))
    acc = more_keys(dev, near_tokens, acc, first, (a1h, a3l, b1h, b3l))
    second = ((0, 1, 0), (0, 3, 1), (512, 1, 0), (512, 3, 1))
    acc = more_keys(dev, near_tokens, acc, second, (a1l, a3h, b1l, b3h))
    acc = more_keys(dev, near_tokens, acc, ((512, 2, 0), (512, 2, 1)), far_x)
    pooled = attend(
        dev,
        lengths,
        near_tokens,
        acc,
        sums,
        far_z,
        both,
        *tables,
    )
    pooled = exchanged(pooled, "fsdp")
    attn = mix(pooled, both, w_out[0])
    attn = exchanged(attn, "fsdp")
    m_norm, after_attn = middle(attn, own_last, gain_mlp)
    m_norm = exchanged(m_norm, "fsdp")
    down = mlp(m_norm, w_gate[0].T, w_up[0].T, w_down[0])
    down = exchanged(down, "fsdp")

    cols = finish(down, after_attn, gain_final, reward_head, judges * devices)
    cols = exchanged(cols, ("judge", "fsdp"))
    mean = jnp.sum(cols.reshape(judges, devices, 384), axis=0) / judges
    total_cols = mean[:, :256].reshape(cands, 128)
    panel = mean[:, 256 : 256 + seq_dev].reshape(cands)
    weight_values, panel_member = remaining_candidates(
        panel, duplicate_group_index, duplicate_groups
    )
    cluster_cols = jnp.dot(
        panel_member.T, weight_values[:, None] * total_cols, precision=lax.Precision.HIGHEST
    )
    return (weight_values, cluster_cols)


def solution(mesh):
    in_specs = (
        P("judge", "fsdp", None),
        P(),
        P(),
        P("judge", "fsdp"),
        P("judge", None, "fsdp"),
        P("judge", "fsdp", None),
        P("judge", "fsdp", None),
        P("judge", "fsdp", None),
        P("judge", "fsdp"),
        P("judge", None, "fsdp"),
        P("judge", None, "fsdp"),
        P("judge", "fsdp", None),
        P("judge", "fsdp"),
        P("judge", None),
    )
    out_specs = (P(), P(None, "fsdp"))
    return jax.shard_map(layer, mesh=mesh, in_specs=in_specs, out_specs=out_specs, check_vma=False)
```
